32 devices in a mesh: heads: 2 (over x), ctx: 16 (over z, y, core).
Axes of the slice: x: 2, y: 2, z: 4, core: 2. Of those that a mesh axis runs over, the one named last changes fastest.
Arguments:
- queries: bfloat16 [4096, 4096], P('ctx', 'heads'), may hold values from -80 to 80
- keys: bfloat16 [4096, 1024], P('ctx', 'heads'), may hold values from -4.5 to 4.5
- values: bfloat16 [4096, 1024], P('ctx', 'heads'), may hold values from -6 to 6
- doc_ids: int32 [4096], P('ctx'), may hold values from 0 to 3, never falling along the last dimension, each value on 1 to 2048 neighbouring positions
- out_weight: bfloat16 [4096, 4096], P('heads', 'ctx'), may hold values from -0.09375 to 0.09375
Outputs:
- mixed: bfloat16 [4096, 4096], P('ctx', 'heads')
The draws below stay inside these ranges and needn't reach their ends.
Inputs may be any that keep to these rules, and one draw needn't show every extreme that they name: `doc_ids`: document ids never fall along the tokens; each document has at most 2048 tokens.
All inputs are finite; a program needn't handle non-finite values.
Results may differ from the reference program's by a relative error of at most 0.015.
Values may be sent and summed in bfloat16 or wider, within the bound.
A program may use at most 64 MiB of HBM per device.

```python
import math
import jax
import jax.numpy as jnp
import numpy as np
from jax import lax

D = 4096
QH = 32
KEY_VALUE_HEADS = 8
HEAD_SIZE = 128
LOOKBACK_WINDOW = 4096
TOK_DEV = 256
QPG = 4
SEQUENCE_TOKENS = 4096
MOST_DOC = 2048


def shared_pair(key):
    key_k = jax.random.fold_in(key, 17)
    key_q = jax.random.fold_in(key, 29)
    kbase = jnp.clip(jax.random.normal(key_k, (SEQUENCE_TOKENS, KEY_VALUE_HEADS, HEAD_SIZE), jnp.float32), -4.0, 4.0)
    qbase = jnp.clip(jax.random.normal(key_q, (SEQUENCE_TOKENS, KEY_VALUE_HEADS, QH // KEY_VALUE_HEADS, HEAD_SIZE), jnp.float32), -4.0, 4.0)
    return (qbase, kbase)


def draw_queries(key, part):
    qbase, kbase = shared_pair(key)
    return qbase.reshape(SEQUENCE_TOKENS, QH * HEAD_SIZE).astype(jnp.bfloat16)


def draw_keys(key, part):
    qbase, kbase = shared_pair(key)
    return kbase.reshape(SEQUENCE_TOKENS, KEY_VALUE_HEADS * HEAD_SIZE).astype(jnp.bfloat16)


def block_scale(rng, extent, shards, least, high):
    def one(position, parts):
        draws = jax.random.uniform(jax.random.fold_in(jax.random.fold_in(rng, 6), position), (parts,), jnp.float32, least / len(shards), high / len(shards))
        return jnp.repeat(jnp.exp(draws), extent[position] // parts).reshape((-1,) + (1,) * (len(extent) - position - 1))

    factor_of = one(*shards[0])
    for cut in shards[1:]:
        factor_of = factor_of * one(*cut)
    return factor_of


def split_up(count, total, reach, lean):
    loads = [(1 << 20) // math.isqrt(standing ** lean) + 1 for standing in range(2, count + 1)]
    spare, given = total - reach - (count - 1), [1] * (count - 1)
    while spare > 0:
        movable = [i for i in range(count - 1) if given[i] < reach]
        mass, left = sum([loads[i] for i in movable]), spare
        for i in movable:
            extra = min(reach - given[i], max(1, left * loads[i] // mass), spare)
            given[i] = given[i] + extra
            spare = spare - extra
    return np.array([reach] + given)


def ragged(rng, amount, total, most, lean):
    if amount == 2:
        one = jax.random.randint(rng, (), max(1, total - most), min(most, total - 1) + 1)
        return jnp.stack([one, total - one])
    tallies = jnp.asarray(split_up(amount, total, most, lean), jnp.int32)
    pairs = (amount - 1) // 2
    source_of, receiver = tallies[1:1 + 2 * pairs:2], tallies[2:2 + 2 * pairs:2]
    room = jnp.minimum(source_of - 1, most - receiver)
    passed = jax.random.randint(jax.random.fold_in(rng, 1), (pairs,), 0, 1 << 20) % (room + 1)
    tallies = tallies.at[1:1 + 2 * pairs:2].set(source_of - passed).at[2:2 + 2 * pairs:2].set(receiver + passed)
    return tallies[jax.random.permutation(jax.random.fold_in(rng, 2), amount)]


def bell_draw(rng, extent, spread, bound, cuts=(), kind=jnp.bfloat16):
    entries = jax.random.normal(rng, extent, jnp.float32) * spread
    if len(cuts) > 0:
        entries = block_scale(rng, extent, cuts, -0.22, 0.18) * entries
    return jnp.clip(entries, min=-bound, max=bound).astype(kind)


def setup_inputs(seed: int = 0) -> dict:
    key_list = jax.random.split(jax.random.key(seed), 6)
    queries = draw_queries(jax.random.fold_in(key_list[5], 71), 0)
    keys = draw_keys(jax.random.fold_in(key_list[5], 71), 0)
    values = bell_draw(key_list[2], (SEQUENCE_TOKENS, KEY_VALUE_HEADS * HEAD_SIZE), 1.0, 6.0, ((0, 16), (1, 2)))
    doc_ids = jnp.searchsorted(jnp.cumsum(ragged(key_list[3], SEQUENCE_TOKENS // (4 * TOK_DEV), SEQUENCE_TOKENS, MOST_DOC, 2)), jnp.arange(SEQUENCE_TOKENS), side="right").astype(jnp.int32)
    out_weight = bell_draw(key_list[4], (QH * HEAD_SIZE, D), (QH * HEAD_SIZE) ** -0.5, 0.09375, ((0, 2), (1, 16)))
    return {"queries": queries, "keys": keys, "values": values, "doc_ids": doc_ids, "out_weight": out_weight}


def reference(queries, keys, values, doc_ids, out_weight):
    scale = HEAD_SIZE ** -0.5
    q = queries.reshape(SEQUENCE_TOKENS, KEY_VALUE_HEADS, QPG, HEAD_SIZE)
    kpad = jnp.concatenate([jnp.zeros((LOOKBACK_WINDOW, KEY_VALUE_HEADS * HEAD_SIZE), keys.dtype), keys], axis=0).reshape(SEQUENCE_TOKENS + LOOKBACK_WINDOW, KEY_VALUE_HEADS, HEAD_SIZE)
    value_padded = jnp.concatenate([jnp.zeros((LOOKBACK_WINDOW, KEY_VALUE_HEADS * HEAD_SIZE), values.dtype), values], axis=0).reshape(SEQUENCE_TOKENS + LOOKBACK_WINDOW, KEY_VALUE_HEADS, HEAD_SIZE)
    dpad = jnp.concatenate([jnp.full((LOOKBACK_WINDOW,), -1, jnp.int32), doc_ids.astype(jnp.int32)], axis=0)
    block = TOK_DEV
    window_extent = LOOKBACK_WINDOW + block

    def one(index):
        begin_offset = (index * block).astype(jnp.int32)
        qb = lax.dynamic_slice_in_dim(q, begin_offset, block, 0).astype(jnp.float32)
        kb = lax.dynamic_slice_in_dim(kpad, begin_offset, window_extent, 0).astype(jnp.float32)
        value_block = lax.dynamic_slice_in_dim(value_padded, begin_offset, window_extent, 0).astype(jnp.float32)
        dq = lax.dynamic_slice_in_dim(doc_ids.astype(jnp.int32), begin_offset, block, 0)
        dk = lax.dynamic_slice_in_dim(dpad, begin_offset, window_extent, 0)
        scores = jnp.einsum('tgnh,sgh->tgns', qb, kb) * scale
        qpos = begin_offset + jnp.arange(block, dtype=jnp.int32)
        kpos = begin_offset - LOOKBACK_WINDOW + jnp.arange(window_extent, dtype=jnp.int32)
        vis = (kpos[None, :] <= qpos[:, None]) & (qpos[:, None] - kpos[None, :] < LOOKBACK_WINDOW) & (kpos[None, :] >= 0) & (dq[:, None] == dk[None, :])
        vis = vis[:, None, None, :]
        scores = jnp.where(vis, scores, jnp.float32(-1e30))
        rowmax = jnp.max(scores, axis=-1, keepdims=True)
        weights = jnp.where(vis, jnp.exp(scores - rowmax), jnp.float32(0.0))
        total = jnp.sum(weights, axis=-1)
        rounded = weights.astype(jnp.bfloat16)
        out = jnp.einsum('tgns,sgh->tgnh', rounded.astype(jnp.float32), value_block) / total[..., None]
        return out.astype(jnp.bfloat16).reshape(block, KEY_VALUE_HEADS * QPG * HEAD_SIZE)

    attn = lax.map(one, jnp.arange(SEQUENCE_TOKENS // block, dtype=jnp.int32)).reshape(SEQUENCE_TOKENS, QH * HEAD_SIZE)
    return jnp.dot(attn, out_weight, preferred_element_type=jnp.float32).astype(jnp.bfloat16)
```

```python
import functools
import math

import jax
import jax.numpy as jnp
from jax import lax
from jax.experimental import pallas as pl
from jax.experimental.pallas import tpu as pltpu
from jax.sharding import PartitionSpec as P

HEAD_SIZE = 128
LOOKBACK_WINDOW = 4096
QPG = 4


PLANE = 4
DOC_ROWS = 16
MESH = pl.DeviceIdType.MESH


def fused_kernel(
    planes, n_heads, groups, tok, wcols,
    q_ref, kv_hbm, w_hbm, out_ref,
    kvbuf, wbuf, abuf, acc, rowmax, total, bias, xsend, xrecv, keep, rsend, obuf,
    local_sem, kv_recv, kvz_send, kvp_send, kvf_send,
    w_recv, w_right, w_left, a_recv, a_send, a_fwd,
    x_send, x_recv, o_send, o_recv,
):
    h = lax.axis_index("heads")
    c = lax.axis_index("ctx")
    z = c // PLANE
    p = c % PLANE
    core = p % 2
    row = p // 2
    mate = p + 1 - 2 * core
    across = (p + 2) % PLANE
    diag = (mate + 2) % PLANE
    last = planes - 1
    kdim = groups * HEAD_SIZE
    span = QPG * groups
    per_half = planes // n_heads

    def in_plane(other):
        return (h, z * PLANE + other)

    up = (h, c + PLANE)
    down = (h, c - PLANE)

    def copy(src, dst, send, recv, dev):
        return pltpu.make_async_remote_copy(
            src_ref=src, dst_ref=dst, send_sem=send, recv_sem=recv,
            device_id=dev, device_id_type=MESH,
        )

    def kv_up(d):
        return copy(kvbuf.at[d, p], kvbuf.at[d + 1, p], kvz_send.at[d], kv_recv.at[d + 1, p], up)

    def kv_side(d, which):
        dev = in_plane(mate if which == 0 else across)
        return copy(kvbuf.at[d, p], kvbuf.at[d, p], kvp_send.at[d, which], kv_recv.at[d, p], dev)

    def kv_forward(d):
        return copy(
            kvbuf.at[d, across], kvbuf.at[d, across], kvf_send.at[d], kv_recv.at[d, across],
            in_plane(mate),
        )

    def kv_wait(d, who):
        copy(
            kvbuf.at[d, who], kvbuf.at[d, who], kvf_send.at[d], kv_recv.at[d, who], in_plane(mate)
        ).wait_recv()

    def w_up(j):
        return copy(wbuf.at[j], wbuf.at[j], w_right.at[j], w_recv.at[j], up)

    def w_down(j):
        return copy(wbuf.at[j], wbuf.at[j], w_left.at[j], w_recv.at[j], down)

    def w_wait(j):
        copy(wbuf.at[j], wbuf.at[j], w_left.at[j], w_recv.at[j], in_plane(mate)).wait_recv()

    def a_side(which):
        dev = in_plane(mate if which == 0 else across)
        return copy(abuf.at[p], abuf.at[p], a_send.at[which], a_recv.at[p], dev)

    def a_forward():
        return copy(abuf.at[across], abuf.at[across], a_fwd, a_recv.at[across], in_plane(mate))

    def a_wait(who):
        copy(abuf.at[who], abuf.at[who], a_fwd, a_recv.at[who], in_plane(mate)).wait_recv()

    def x_copy(jj, pp):
        return copy(
            xsend.at[jj, pp], xrecv.at[jj, pp], x_send.at[jj, pp], x_recv.at[jj, pp], (1 - h, c)
        )

    def o_copy(jj, pp):
        return copy(
            rsend.at[jj, pp], obuf.at[jj, p], o_send.at[jj, pp], o_recv.at[jj, p], in_plane(pp)
        )

    kv_in = pltpu.make_async_copy(kv_hbm, kvbuf.at[0, p], local_sem.at[0])
    w_in = pltpu.make_async_copy(w_hbm, wbuf.at[z], local_sem.at[1])
    kv_in.start()
    w_in.start()

    barrier = pltpu.get_barrier_semaphore()
    for dev in (in_plane(mate), in_plane(across), in_plane(diag), (1 - h, c)):
        pl.semaphore_signal(barrier, inc=1, device_id=dev, device_id_type=MESH)

    @pl.when(z < last)
    def _():
        pl.semaphore_signal(barrier, inc=1, device_id=up, device_id_type=MESH)

    @pl.when(z > 0)
    def _():
        pl.semaphore_signal(barrier, inc=1, device_id=down, device_id_type=MESH)

    pl.semaphore_wait(barrier, 4 + jnp.minimum(z, 1) + jnp.minimum(last - z, 1))

    kv_in.wait()

    @pl.when(z < last)
    def _():
        kv_up(0).start()

    @pl.when(row == 0)
    def _():
        kv_side(0, 1).start()

    @pl.when(core == 0)
    def _():
        kv_side(0, 0).start()

    w_in.wait()

    @pl.when(z > 0)
    def _():
        w_down(z).start()

    factor = HEAD_SIZE ** (-0.5) * math.log2(math.e)

    def docs_of(block):
        return block[tok : tok + DOC_ROWS, 0:tok].astype(jnp.float32)[0:1, :]

    def attend(d, who, first):
        block = kvbuf.at[d, who]
        kdoc = jnp.broadcast_to(docs_of(block), (tok, tok)).T
        vis = kdoc == docs_of(kvbuf.at[0, p])
        if first:
            kpos = lax.broadcasted_iota(jnp.int32, (tok, tok), 0)
            qpos = lax.broadcasted_iota(jnp.int32, (tok, tok), 1)
            vis = vis & (kpos <= qpos)
        bias[...] = jnp.where(vis, jnp.float32(0.0), jnp.float32(-1e30))

        def group(g, carry):
            keys = block[0:tok, pl.ds(pl.multiple_of(g * HEAD_SIZE, HEAD_SIZE), HEAD_SIZE)]
            vals = block[0:tok, pl.ds(pl.multiple_of(kdim + g * HEAD_SIZE, HEAD_SIZE), HEAD_SIZE)]
            for n in range(QPG):
                head = g * QPG + n
                qs = q_ref[:, pl.ds(pl.multiple_of(head * HEAD_SIZE, HEAD_SIZE), HEAD_SIZE)]
                scores = lax.dot_general(
                    keys, qs, (((1,), (1,)), ((), ())), preferred_element_type=jnp.float32
                ) + bias[...]
                top = jnp.max(scores, axis=0, keepdims=True)
                if not first:
                    old = rowmax[head]
                    top = jnp.maximum(old, top)
                weights = jnp.exp2((scores - top) * factor)
                sums = jnp.sum(weights, axis=0, keepdims=True)
                contrib = lax.dot_general(
                    vals, weights.astype(jnp.bfloat16), (((0,), (0,)), ((), ())),
                    preferred_element_type=jnp.float32,
                )
                if first:
                    total[head] = sums
                    acc[head] = contrib
                else:
                    shrink = jnp.exp2((old - top) * factor)
                    total[head] = total[head] * shrink + sums
                    acc[head] = acc[head] * shrink + contrib
                rowmax[head] = top
            return carry

        lax.fori_loop(0, groups, group, 0)

    attend(0, p, True)

    @pl.when(z > 0)
    def _():
        kv_wait(1, p)

        @pl.when(z < last)
        def _():
            kv_up(1).start()

        kv_side(1, 1).start()
        kv_side(1, 0).start()

    @pl.when(z < last)
    def _():
        w_up(z).start()

    @pl.when(row == 1)
    def _():
        kv_wait(0, across)
        kv_forward(0).start()

    @pl.when(core == 1)
    def _():
        kv_wait(0, mate)

    @pl.when(row == 1)
    def _():
        kv_wait(0, diag)

    def block_loop(d, lo, hi):
        def one(who, carry):
            attend(d, who, False)
            return carry

        lax.fori_loop(lo, hi, one, 0)

    block_loop(0, 0, p)

    @pl.when(z > 0)
    def _():
        kv_wait(1, across)
        kv_forward(1).start()

    @pl.when(z > 1)
    def _():
        kv_wait(2, p)

        @pl.when(row == 1)
        def _():
            kv_side(2, 1).start()

        @pl.when(core == 1)
        def _():
            kv_side(2, 0).start()

    @pl.when(z < last)
    def _():
        w_wait(z + 1)

        @pl.when(z > 0)
        def _():
            w_down(z + 1).start()

    @pl.when(z > 0)
    def _():
        kv_wait(1, mate)
        kv_wait(1, diag)
        block_loop(1, 0, PLANE)

    @pl.when(z > 1)
    def _():
        @pl.when(row == 0)
        def _():
            kv_wait(2, across)
            kv_forward(2).start()

        @pl.when(core == 0)
        def _():
            kv_wait(2, mate)

        @pl.when(row == 0)
        def _():
            kv_wait(2, diag)

        block_loop(2, p, PLANE)

    def finish_head(head, carry):
        cols = pl.ds(pl.multiple_of(head * HEAD_SIZE, HEAD_SIZE), HEAD_SIZE)
        abuf[p, :, cols] = (acc[head] / total[head]).T.astype(jnp.bfloat16)
        return carry

    lax.fori_loop(0, span, finish_head, 0)
    a_side(1).start()
    a_side(0).start()

    @pl.when(z > 0)
    def _():
        w_wait(z - 1)

        @pl.when(z < last)
        def _():
            w_up(z - 1).start()

    @pl.when(z + 2 < planes)
    def _():
        w_wait(z + 2)

        @pl.when(z > 0)
        def _():
            w_down(z + 2).start()

    a_wait(across)
    a_forward().start()
    a_wait(mate)
    a_wait(diag)

    def plane_of(i):
        dist = (i + 1) // 2
        return z + dist * (2 * (i % 2) - 1)

    def project(i):
        j = plane_of(i)

        @pl.when((j >= 0) & (j < planes))
        def _():
            @pl.when(i >= 4)
            def _():
                w_wait(j)

                @pl.when((j < z) & (z < last))
                def _():
                    w_up(j).start()

                @pl.when((j > z) & (z > 0))
                def _():
                    w_down(j).start()

            jj = j % per_half
            mine = (j // per_half) == h

            def rows(k, carry):
                pp = (p + 1 + k) % PLANE
                part = jnp.dot(abuf[pp], wbuf[j], preferred_element_type=jnp.float32)

                @pl.when(mine)
                def _():
                    keep[jj, pp] = part

                @pl.when(jnp.logical_not(mine))
                def _():
                    xsend[jj, pp] = part.astype(jnp.bfloat16)
                    x_copy(jj, pp).start()

                return carry

            lax.fori_loop(0, PLANE, rows, 0)

    def finish(i):
        j = plane_of(i)

        @pl.when((j >= 0) & (j < planes) & ((j // per_half) == h))
        def _():
            jj = j % per_half

            def rows(k, carry):
                pp = (p + 1 + k) % PLANE
                x_copy(jj, pp).wait_recv()
                done = (keep[jj, pp] + xrecv[jj, pp].astype(jnp.float32)).astype(jnp.bfloat16)

                @pl.when(pp == p)
                def _():
                    at = pl.multiple_of((jj * PLANE + p) * wcols, wcols)
                    out_ref[:, pl.ds(at, wcols)] = done

                @pl.when(pp != p)
                def _():
                    rsend[jj, pp] = done
                    o_copy(jj, pp).start()

                return carry

            lax.fori_loop(0, PLANE, rows, 0)

    steps = 2 * planes - 1
    project(0)

    def step(i, carry):
        project(i)
        finish(i - 1)
        return carry

    lax.fori_loop(1, steps, step, 0)
    finish(steps - 1)

    def collect(k, carry):
        jj = k // PLANE
        src = k % PLANE

        @pl.when(src != p)
        def _():
            copy(
                obuf.at[jj, src], obuf.at[jj, src], o_send.at[jj, src], o_recv.at[jj, src],
                in_plane(mate),
            ).wait_recv()
            at = pl.multiple_of(k * wcols, wcols)
            out_ref[:, pl.ds(at, wcols)] = obuf[jj, src]
            o_copy(jj, src).wait_send()

        x_copy(jj, src).wait_send()
        return carry

    lax.fori_loop(0, per_half * PLANE, collect, 0)

    a_side(0).wait_send()
    a_side(1).wait_send()
    a_forward().wait_send()

    def w_drain(j, carry):
        @pl.when((j <= z) & (z < last))
        def _():
            w_up(j).wait_send()

        @pl.when((j >= z) & (z > 0))
        def _():
            w_down(j).wait_send()

        return carry

    lax.fori_loop(0, planes, w_drain, 0)

    @pl.when(z < last)
    def _():
        kv_up(0).wait_send()

        @pl.when(z > 0)
        def _():
            kv_up(1).wait_send()

    @pl.when(row == 0)
    def _():
        kv_side(0, 1).wait_send()

    @pl.when(core == 0)
    def _():
        kv_side(0, 0).wait_send()

    @pl.when(row == 1)
    def _():
        kv_forward(0).wait_send()

    @pl.when(z > 0)
    def _():
        kv_side(1, 0).wait_send()
        kv_side(1, 1).wait_send()
        kv_forward(1).wait_send()

    @pl.when(z > 1)
    def _():
        @pl.when(row == 1)
        def _():
            kv_side(2, 1).wait_send()

        @pl.when(core == 1)
        def _():
            kv_side(2, 0).wait_send()

        @pl.when(row == 0)
        def _():
            kv_forward(2).wait_send()


def fused_body(n_ctx, n_heads, queries, keys, values, doc_ids, out_weight):
    tok, qcols = queries.shape
    kdim = keys.shape[1]
    groups = kdim // HEAD_SIZE
    krows, wcols = out_weight.shape
    planes = n_ctx // PLANE
    span = QPG * groups
    per_half = planes // n_heads
    width = 2 * kdim
    docs = jnp.broadcast_to(
        jnp.pad(doc_ids.astype(jnp.bfloat16), (0, width - tok))[None, :], (DOC_ROWS, width)
    )
    kv = jnp.concatenate([jnp.concatenate([keys, values], axis=1), docs], axis=0)
    bf, f32 = jnp.bfloat16, jnp.float32
    dma = pltpu.SemaphoreType.DMA
    return pl.pallas_call(
        functools.partial(fused_kernel, planes, n_heads, groups, tok, wcols),
        out_shape=jax.ShapeDtypeStruct((tok, per_half * PLANE * wcols), bf),
        in_specs=[
            pl.BlockSpec(memory_space=pltpu.VMEM),
            pl.BlockSpec(memory_space=pl.ANY),
            pl.BlockSpec(memory_space=pl.ANY),
        ],
        out_specs=pl.BlockSpec(memory_space=pltpu.VMEM),
        scratch_shapes=[
            pltpu.VMEM((3, PLANE, tok + DOC_ROWS, width), bf),
            pltpu.VMEM((planes, krows, wcols), bf),
            pltpu.VMEM((PLANE, tok, krows), bf),
            pltpu.VMEM((span, HEAD_SIZE, tok), f32),
            pltpu.VMEM((span, 1, tok), f32),
            pltpu.VMEM((span, 1, tok), f32),
            pltpu.VMEM((tok, tok), f32),
            pltpu.VMEM((per_half, PLANE, tok, wcols), bf),
            pltpu.VMEM((per_half, PLANE, tok, wcols), bf),
            pltpu.VMEM((per_half, PLANE, tok, wcols), f32),
            pltpu.VMEM((per_half, PLANE, tok, wcols), bf),
            pltpu.VMEM((per_half, PLANE, tok, wcols), bf),
            dma((2,)),
            dma((3, PLANE)),
            dma((2,)),
            dma((3, 2)),
            dma((3,)),
            dma((planes,)),
            dma((planes,)),
            dma((planes,)),
            dma((PLANE,)),
            dma((2,)),
            dma,
            dma((per_half, PLANE)),
            dma((per_half, PLANE)),
            dma((per_half, PLANE)),
            dma((per_half, PLANE)),
        ],
        compiler_params=pltpu.CompilerParams(
            collective_id=0, has_side_effects=True, vmem_limit_bytes=56 * 1024 * 1024
        ),
    )(queries, kv, out_weight)


def fits_fused(n_ctx, n_heads, queries, keys, out_weight):
    tokens = queries.shape[0]
    tok = tokens // n_ctx
    reach = min(LOOKBACK_WINDOW, tokens // 2)
    return (
        n_heads == 2
        and n_ctx % PLANE == 0
        and n_ctx // PLANE == 4
        and tok == 2 * HEAD_SIZE
        and reach == 2 * PLANE * tok
        and reach < LOOKBACK_WINDOW
        and 2 * keys.shape[1] // n_heads >= tok
        and (out_weight.shape[1] // n_ctx) % 128 == 0
        and keys.shape[1] // n_heads % HEAD_SIZE == 0
    )


def passed_along(block, axis, distance):
    devices = range(lax.axis_size(axis))
    route = [(i - distance, i) for i in devices if i - distance in devices]
    return lax.ppermute(block, axis, route)


def body(queries, keys, values, doc_ids, out_weight):
    tok_rows = queries.shape[0]
    groups = keys.shape[1] // HEAD_SIZE
    scale = HEAD_SIZE ** (-0.5)
    q_local = queries.reshape(tok_rows, groups, QPG, HEAD_SIZE)
    here = lax.axis_index("ctx")
    qpos = here * tok_rows + jnp.arange(tok_rows, dtype=jnp.int32)
    reach = LOOKBACK_WINDOW // tok_rows

    def work(state, kblk, vblk, sblk, kstart):
        rowmax, total, accum = state
        scores = (
            jnp.einsum(
                "tgnh,sgh->tgns",
                q_local,
                kblk.reshape(tok_rows, groups, HEAD_SIZE),
                preferred_element_type=jnp.float32,
            )
            * scale
        )
        kpos = kstart + jnp.arange(tok_rows, dtype=jnp.int32)
        vis = (
            (kpos[None, :] <= qpos[:, None])
            & (qpos[:, None] - kpos[None, :] < LOOKBACK_WINDOW)
            & (kpos[None, :] >= 0)
            & (doc_ids[:, None] == sblk[None, :])
        )
        vis = vis[:, None, None, :]
        scores = jnp.where(vis, scores, jnp.float32(-1e30))
        newmax = jnp.maximum(rowmax, jnp.max(scores, axis=-1))
        weights = jnp.where(vis, jnp.exp(scores - newmax[..., None]), jnp.float32(0.0))
        factor = jnp.exp(rowmax - newmax)
        total = total * factor + jnp.sum(weights, axis=-1)
        rounded = weights.astype(jnp.bfloat16)
        contrib = jnp.einsum(
            "tgns,sgh->tgnh",
            rounded,
            vblk.reshape(tok_rows, groups, HEAD_SIZE),
            preferred_element_type=jnp.float32,
        )
        accum = accum * factor[..., None] + contrib
        return (newmax, total, accum)

    def attend(state, kblk, vblk, sblk, kstart):
        return work(state, kblk, vblk, sblk, kstart)

    state = (
        jnp.full((tok_rows, groups, QPG), -1e30, jnp.float32),
        jnp.zeros((tok_rows, groups, QPG), jnp.float32),
        jnp.zeros((tok_rows, groups, QPG, HEAD_SIZE), jnp.float32),
    )
    state = attend(state, keys, values, doc_ids, here * tok_rows)

    def chain_step(depth, carry):
        st, kblk, vblk, sblk = carry
        kblk, vblk, sblk = passed_along((kblk, vblk, sblk), "ctx", 1)
        st = attend(st, kblk, vblk, sblk, (here - depth) * tok_rows)
        return (st, kblk, vblk, sblk)

    state = lax.fori_loop(1, reach + 1, chain_step, (state, keys, values, doc_ids))[0]
    rowmax, total, accum = state
    attn = (
        (accum / total[..., None]).astype(jnp.bfloat16).reshape(tok_rows, groups * QPG * HEAD_SIZE)
    )
    partial_sums = jnp.dot(
        attn,
        lax.all_gather(out_weight, "ctx", axis=1, tiled=True),
        preferred_element_type=jnp.float32,
    )
    return lax.psum_scatter(
        partial_sums.astype(jnp.bfloat16), "heads", scatter_dimension=1, tiled=True
    )


def solution(mesh):
    in_specs = (
        P("ctx", "heads"),
        P("ctx", "heads"),
        P("ctx", "heads"),
        P("ctx"),
        P("heads", "ctx"),
    )
    out_specs = P("ctx", "heads")

    def run(queries, keys, values, doc_ids, out_weight):
        n_ctx, n_heads = mesh.shape["ctx"], mesh.shape["heads"]
        local = body
        if fits_fused(n_ctx, n_heads, queries, keys, out_weight):
            local = functools.partial(fused_body, n_ctx, n_heads)
        return jax.shard_map(
            local, mesh=mesh, in_specs=in_specs, out_specs=out_specs, check_vma=False
        )(queries, keys, values, doc_ids, out_weight)

    return run
```

```python
import functools
import math

import jax
import jax.numpy as jnp
from jax import lax
from jax.experimental import pallas as pl
from jax.experimental.pallas import tpu as pltpu
from jax.sharding import PartitionSpec as P

HEAD_SIZE = 128
LOOKBACK_WINDOW = 4096
QPG = 4


PLANE = 4
DOC_ROWS = 16
MESH = pl.DeviceIdType.MESH


def fused_kernel(
    planes, n_heads, groups, tok, wcols,
    q_ref, kv_hbm, w_hbm, out_ref,
    kvbuf, wbuf, abuf, acc, rowmax, total, bias, xsend, xrecv, keep, rsend, obuf,
    local_sem, kv_recv, kvz_send, kvp_send, kvf_send,
    w_recv, w_right, w_left, a_recv, a_send, a_fwd,
    x_send, x_recv, o_send, o_recv,
):
    h = lax.axis_index("heads")
    c = lax.axis_index("ctx")
    z = c // PLANE
    p = c % PLANE
    core = p % 2
    row = p // 2
    mate = p + 1 - 2 * core
    across = (p + 2) % PLANE
    diag = (mate + 2) % PLANE
    last = planes - 1
    kdim = groups * HEAD_SIZE
    span = QPG * groups
    per_half = planes // n_heads
    half = wcols // 2

    def in_plane(other):
        return (h, z * PLANE + other)

    up = (h, c + PLANE)
    down = (h, c - PLANE)

    def copy(src, dst, send, recv, dev):
        return pltpu.make_async_remote_copy(
            src_ref=src, dst_ref=dst, send_sem=send, recv_sem=recv,
            device_id=dev, device_id_type=MESH,
        )

    def kv_up(d):
        return copy(kvbuf.at[d, p], kvbuf.at[d + 1, p], kvz_send.at[d], kv_recv.at[d + 1, p], up)

    def kv_side(d, which):
        dev = in_plane(mate if which == 0 else across)
        return copy(kvbuf.at[d, p], kvbuf.at[d, p], kvp_send.at[d, which], kv_recv.at[d, p], dev)

    def kv_forward(d):
        return copy(
            kvbuf.at[d, across], kvbuf.at[d, across], kvf_send.at[d], kv_recv.at[d, across],
            in_plane(mate),
        )

    def kv_wait(d, who):
        copy(
            kvbuf.at[d, who], kvbuf.at[d, who], kvf_send.at[d], kv_recv.at[d, who], in_plane(mate)
        ).wait_recv()

    def w_up(j, s):
        ref = wbuf.at[j, s]
        return copy(ref, ref, w_right.at[j, s], w_recv.at[j, s], up)

    def w_down(j, s):
        ref = wbuf.at[j, s]
        return copy(ref, ref, w_left.at[j, s], w_recv.at[j, s], down)

    def w_wait(j, s):
        ref = wbuf.at[j, s]
        copy(ref, ref, w_left.at[j, s], w_recv.at[j, s], in_plane(mate)).wait_recv()

    def w_from_above(j):
        for s in range(2):
            w_wait(j, s)

            @pl.when(z > 0)
            def _():
                w_down(j, s).start()

    def w_from_below(j):
        for s in range(2):
            w_wait(j, s)

            @pl.when(z < last)
            def _():
                w_up(j, s).start()

    def target(k):
        return jnp.where(k == 0, across, jnp.where(k == 1, diag, jnp.where(k == 2, mate, p)))

    def a_side(which):
        dev = in_plane(mate if which == 0 else across)
        return copy(abuf.at[p], abuf.at[p], a_send.at[which], a_recv.at[p], dev)

    def a_forward():
        return copy(abuf.at[across], abuf.at[across], a_fwd, a_recv.at[across], in_plane(mate))

    def a_wait(who):
        copy(abuf.at[who], abuf.at[who], a_fwd, a_recv.at[who], in_plane(mate)).wait_recv()

    def x_copy(u, pp):
        return copy(
            xsend.at[u, pp], xrecv.at[u, pp], x_send.at[u, pp], x_recv.at[u, pp], (1 - h, c)
        )

    def o_copy(u, pp):
        return copy(
            rsend.at[u, pp], obuf.at[u, p], o_send.at[u, pp], o_recv.at[u, p], in_plane(pp)
        )

    kv_in = pltpu.make_async_copy(kv_hbm, kvbuf.at[0, p], local_sem.at[0])
    w_in = [
        pltpu.make_async_copy(
            w_hbm.at[:, s * half : (s + 1) * half], wbuf.at[z, s], local_sem.at[1 + s]
        )
        for s in range(2)
    ]
    kv_in.start()
    w_in[0].start()
    w_in[1].start()

    barrier = pltpu.get_barrier_semaphore()
    for dev in (in_plane(mate), in_plane(across), in_plane(diag), (1 - h, c)):
        pl.semaphore_signal(barrier, inc=1, device_id=dev, device_id_type=MESH)

    @pl.when(z < last)
    def _():
        pl.semaphore_signal(barrier, inc=1, device_id=up, device_id_type=MESH)

    @pl.when(z > 0)
    def _():
        pl.semaphore_signal(barrier, inc=1, device_id=down, device_id_type=MESH)

    pl.semaphore_wait(barrier, 4 + jnp.minimum(z, 1) + jnp.minimum(last - z, 1))

    kv_in.wait()

    @pl.when(z < last)
    def _():
        kv_up(0).start()

    @pl.when(row == 0)
    def _():
        kv_side(0, 1).start()

    @pl.when(core == 0)
    def _():
        kv_side(0, 0).start()

    w_in[0].wait()
    w_in[1].wait()

    @pl.when(z > 0)
    def _():
        w_down(z, 0).start()
        w_down(z, 1).start()

    factor = HEAD_SIZE ** (-0.5) * math.log2(math.e)

    def docs_of(block):
        return block[tok : tok + DOC_ROWS, 0:tok].astype(jnp.float32)[0:1, :]

    def attend(d, who, first):
        block = kvbuf.at[d, who]
        kdoc = jnp.broadcast_to(docs_of(block), (tok, tok)).T
        vis = kdoc == docs_of(kvbuf.at[0, p])
        if first:
            kpos = lax.broadcasted_iota(jnp.int32, (tok, tok), 0)
            qpos = lax.broadcasted_iota(jnp.int32, (tok, tok), 1)
            vis = vis & (kpos <= qpos)
        bias[...] = jnp.where(vis, jnp.float32(0.0), jnp.float32(-1e30))

        def group(g, carry):
            keys = block[0:tok, pl.ds(pl.multiple_of(g * HEAD_SIZE, HEAD_SIZE), HEAD_SIZE)]
            vals = block[0:tok, pl.ds(pl.multiple_of(kdim + g * HEAD_SIZE, HEAD_SIZE), HEAD_SIZE)]
            for n in range(QPG):
                head = g * QPG + n
                qs = q_ref[:, pl.ds(pl.multiple_of(head * HEAD_SIZE, HEAD_SIZE), HEAD_SIZE)]
                scores = lax.dot_general(
                    keys, qs, (((1,), (1,)), ((), ())), preferred_element_type=jnp.float32
                ) + bias[...]
                top = jnp.max(scores, axis=0, keepdims=True)
                if not first:
                    old = rowmax[head]
                    top = jnp.maximum(old, top)
                weights = jnp.exp2((scores - top) * factor)
                sums = jnp.sum(weights, axis=0, keepdims=True)
                contrib = lax.dot_general(
                    vals, weights.astype(jnp.bfloat16), (((0,), (0,)), ((), ())),
                    preferred_element_type=jnp.float32,
                )
                if first:
                    total[head] = sums
                    acc[head] = contrib
                else:
                    shrink = jnp.exp2((old - top) * factor)
                    total[head] = total[head] * shrink + sums
                    acc[head] = acc[head] * shrink + contrib
                rowmax[head] = top
            return carry

        lax.fori_loop(0, groups, group, 0)

    attend(0, p, True)

    @pl.when(z > 0)
    def _():
        kv_wait(1, p)

        @pl.when(z < last)
        def _():
            kv_up(1).start()

        kv_side(1, 1).start()
        kv_side(1, 0).start()

    @pl.when(z < last)
    def _():
        w_up(z, 0).start()
        w_up(z, 1).start()

    @pl.when(row == 1)
    def _():
        kv_wait(0, across)
        kv_forward(0).start()

    @pl.when(core == 1)
    def _():
        kv_wait(0, mate)

    @pl.when(row == 1)
    def _():
        kv_wait(0, diag)

    def block_loop(d, lo, hi):
        def one(who, carry):
            attend(d, who, False)
            return carry

        lax.fori_loop(lo, hi, one, 0)

    block_loop(0, 0, p)

    @pl.when(z > 0)
    def _():
        kv_wait(1, across)
        kv_forward(1).start()

    @pl.when(z > 1)
    def _():
        kv_wait(2, p)

        @pl.when(row == 1)
        def _():
            kv_side(2, 1).start()

        @pl.when(core == 1)
        def _():
            kv_side(2, 0).start()

    @pl.when(z < last)
    def _():
        w_from_above(z + 1)

    @pl.when(z > 0)
    def _():
        kv_wait(1, mate)
        kv_wait(1, diag)
        block_loop(1, 0, PLANE)

    @pl.when(z > 0)
    def _():
        w_from_below(z - 1)

    @pl.when(z + 2 < planes)
    def _():
        w_from_above(z + 2)

    @pl.when(z > 1)
    def _():
        @pl.when(row == 0)
        def _():
            kv_wait(2, across)
            kv_forward(2).start()

        @pl.when(core == 0)
        def _():
            kv_wait(2, mate)

        @pl.when(row == 0)
        def _():
            kv_wait(2, diag)

        block_loop(2, p, PLANE)

    def finish_head(head, carry):
        cols = pl.ds(pl.multiple_of(head * HEAD_SIZE, HEAD_SIZE), HEAD_SIZE)
        abuf[p, :, cols] = (acc[head] / total[head]).T.astype(jnp.bfloat16)
        return carry

    lax.fori_loop(0, span, finish_head, 0)
    a_side(1).start()
    a_side(0).start()

    @pl.when(z > 1)
    def _():
        w_from_below(z - 2)

    a_wait(across)
    a_forward().start()
    a_wait(mate)
    a_wait(diag)

    def plane_of(i):
        dist = (i + 1) // 2
        return z + dist * (2 * (i % 2) - 1)

    def exists(j):
        return (j >= 0) & (j < planes)

    def place(u, pp, part):
        j = u // 2
        mine = (j // per_half) == h
        uu = u % (2 * per_half)

        @pl.when(mine)
        def _():
            keep[uu, pp] = part

        @pl.when(jnp.logical_not(mine))
        def _():
            xsend[uu, pp] = part.astype(jnp.bfloat16)
            x_copy(uu, pp).start()

    def project(i):
        j = plane_of(i)

        @pl.when(exists(j))
        def _():
            @pl.when(i >= 5)
            def _():
                w_wait(j, 0)
                w_wait(j, 1)

            def rows(k, carry):
                pp = target(k)
                both = jnp.concatenate([wbuf[j, 0], wbuf[j, 1]], axis=1)
                part = jnp.dot(abuf[pp], both, preferred_element_type=jnp.float32)
                place(2 * j, pp, part[:, :half])
                place(2 * j + 1, pp, part[:, half:])
                return carry

            lax.fori_loop(0, PLANE, rows, 0)

    def project_half(i, s):
        j = plane_of(i)

        @pl.when(exists(j))
        def _():
            w_wait(j, s)

            def rows(k, carry):
                pp = target(k)
                part = jnp.dot(abuf[pp], wbuf[j, s], preferred_element_type=jnp.float32)
                place(2 * j + s, pp, part)
                return carry

            lax.fori_loop(0, PLANE, rows, 0)

    def finish(i, s):
        j = plane_of(i)

        @pl.when(exists(j) & ((j // per_half) == h))
        def _():
            u = (2 * j + s) % (2 * per_half)

            def rows(k, carry):
                pp = target(k)
                x_copy(u, pp).wait_recv()
                done = (keep[u, pp] + xrecv[u, pp].astype(jnp.float32)).astype(jnp.bfloat16)

                @pl.when(pp == p)
                def _():
                    out_ref[:, column(u, p)] = done

                @pl.when(pp != p)
                def _():
                    rsend[u, pp] = done
                    o_copy(u, pp).start()

                return carry

            lax.fori_loop(0, PLANE, rows, 0)

    def column(u, src):
        return pl.ds(pl.multiple_of(((u // 2) * PLANE + src) * wcols + (u % 2) * half, half), half)

    steps = 2 * planes - 1

    def project_step(i, carry):
        project(i)
        return carry

    def finish_step(k, carry):
        finish(k // 2, k % 2)
        return carry

    lax.fori_loop(0, steps - 1, project_step, 0)
    lax.fori_loop(0, 2 * (steps - 1), finish_step, 0)

    def far_project(s, carry):
        project_half(steps - 1, s)
        return carry

    lax.fori_loop(0, 2, far_project, 0)
    lax.fori_loop(2 * (steps - 1), 2 * steps, finish_step, 0)

    def collect(k, carry):
        u = k // PLANE
        src = k % PLANE

        @pl.when(src != p)
        def _():
            copy(
                obuf.at[u, src], obuf.at[u, src], o_send.at[u, src], o_recv.at[u, src],
                in_plane(mate),
            ).wait_recv()
            out_ref[:, column(u, src)] = obuf[u, src]
            o_copy(u, src).wait_send()

        x_copy(u, src).wait_send()
        return carry

    lax.fori_loop(0, 2 * per_half * PLANE, collect, 0)

    a_side(0).wait_send()
    a_side(1).wait_send()
    a_forward().wait_send()

    def w_drain(j, carry):
        @pl.when((j <= z) & (z < last))
        def _():
            w_up(j, 0).wait_send()
            w_up(j, 1).wait_send()

        @pl.when((j >= z) & (z > 0))
        def _():
            w_down(j, 0).wait_send()
            w_down(j, 1).wait_send()

        return carry

    lax.fori_loop(0, planes, w_drain, 0)

    @pl.when(z < last)
    def _():
        kv_up(0).wait_send()

        @pl.when(z > 0)
        def _():
            kv_up(1).wait_send()

    @pl.when(row == 0)
    def _():
        kv_side(0, 1).wait_send()

    @pl.when(core == 0)
    def _():
        kv_side(0, 0).wait_send()

    @pl.when(row == 1)
    def _():
        kv_forward(0).wait_send()

    @pl.when(z > 0)
    def _():
        kv_side(1, 0).wait_send()
        kv_side(1, 1).wait_send()
        kv_forward(1).wait_send()

    @pl.when(z > 1)
    def _():
        @pl.when(row == 1)
        def _():
            kv_side(2, 1).wait_send()

        @pl.when(core == 1)
        def _():
            kv_side(2, 0).wait_send()

        @pl.when(row == 0)
        def _():
            kv_forward(2).wait_send()


def fused_body(n_ctx, n_heads, queries, keys, values, doc_ids, out_weight):
    tok, qcols = queries.shape
    kdim = keys.shape[1]
    groups = kdim // HEAD_SIZE
    krows, wcols = out_weight.shape
    planes = n_ctx // PLANE
    span = QPG * groups
    per_half = planes // n_heads
    width = 2 * kdim
    docs = jnp.broadcast_to(
        jnp.pad(doc_ids.astype(jnp.bfloat16), (0, width - tok))[None, :], (DOC_ROWS, width)
    )
    kv = jnp.concatenate([jnp.concatenate([keys, values], axis=1), docs], axis=0)
    bf, f32 = jnp.bfloat16, jnp.float32
    dma = pltpu.SemaphoreType.DMA
    return pl.pallas_call(
        functools.partial(fused_kernel, planes, n_heads, groups, tok, wcols),
        out_shape=jax.ShapeDtypeStruct((tok, per_half * PLANE * wcols), bf),
        in_specs=[
            pl.BlockSpec(memory_space=pltpu.VMEM),
            pl.BlockSpec(memory_space=pl.ANY),
            pl.BlockSpec(memory_space=pl.ANY),
        ],
        out_specs=pl.BlockSpec(memory_space=pltpu.VMEM),
        scratch_shapes=[
            pltpu.VMEM((3, PLANE, tok + DOC_ROWS, width), bf),
            pltpu.VMEM((planes, 2, krows, wcols // 2), bf),
            pltpu.VMEM((PLANE, tok, krows), bf),
            pltpu.VMEM((span, HEAD_SIZE, tok), f32),
            pltpu.VMEM((span, 1, tok), f32),
            pltpu.VMEM((span, 1, tok), f32),
            pltpu.VMEM((tok, tok), f32),
            pltpu.VMEM((2 * per_half, PLANE, tok, wcols // 2), bf),
            pltpu.VMEM((2 * per_half, PLANE, tok, wcols // 2), bf),
            pltpu.VMEM((2 * per_half, PLANE, tok, wcols // 2), f32),
            pltpu.VMEM((2 * per_half, PLANE, tok, wcols // 2), bf),
            pltpu.VMEM((2 * per_half, PLANE, tok, wcols // 2), bf),
            dma((3,)),
            dma((3, PLANE)),
            dma((2,)),
            dma((3, 2)),
            dma((3,)),
            dma((planes, 2)),
            dma((planes, 2)),
            dma((planes, 2)),
            dma((PLANE,)),
            dma((2,)),
            dma,
            dma((2 * per_half, PLANE)),
            dma((2 * per_half, PLANE)),
            dma((2 * per_half, PLANE)),
            dma((2 * per_half, PLANE)),
        ],
        compiler_params=pltpu.CompilerParams(
            collective_id=0, has_side_effects=True, vmem_limit_bytes=56 * 1024 * 1024
        ),
    )(queries, kv, out_weight)


def fits_fused(n_ctx, n_heads, queries, keys, out_weight):
    tokens = queries.shape[0]
    tok = tokens // n_ctx
    reach = min(LOOKBACK_WINDOW, tokens // 2)
    return (
        n_heads == 2
        and n_ctx % PLANE == 0
        and n_ctx // PLANE == 4
        and tok == 2 * HEAD_SIZE
        and reach == 2 * PLANE * tok
        and reach < LOOKBACK_WINDOW
        and 2 * keys.shape[1] // n_heads >= tok
        and (out_weight.shape[1] // n_ctx) % 256 == 0
        and keys.shape[1] // n_heads % HEAD_SIZE == 0
    )


def passed_along(block, axis, distance):
    devices = range(lax.axis_size(axis))
    route = [(i - distance, i) for i in devices if i - distance in devices]
    return lax.ppermute(block, axis, route)


def body(queries, keys, values, doc_ids, out_weight):
    tok_rows = queries.shape[0]
    groups = keys.shape[1] // HEAD_SIZE
    scale = HEAD_SIZE ** (-0.5)
    q_local = queries.reshape(tok_rows, groups, QPG, HEAD_SIZE)
    here = lax.axis_index("ctx")
    qpos = here * tok_rows + jnp.arange(tok_rows, dtype=jnp.int32)
    reach = LOOKBACK_WINDOW // tok_rows

    def work(state, kblk, vblk, sblk, kstart):
        rowmax, total, accum = state
        scores = (
            jnp.einsum(
                "tgnh,sgh->tgns",
                q_local,
                kblk.reshape(tok_rows, groups, HEAD_SIZE),
                preferred_element_type=jnp.float32,
            )
            * scale
        )
        kpos = kstart + jnp.arange(tok_rows, dtype=jnp.int32)
        vis = (
            (kpos[None, :] <= qpos[:, None])
            & (qpos[:, None] - kpos[None, :] < LOOKBACK_WINDOW)
            & (kpos[None, :] >= 0)
            & (doc_ids[:, None] == sblk[None, :])
        )
        vis = vis[:, None, None, :]
        scores = jnp.where(vis, scores, jnp.float32(-1e30))
        newmax = jnp.maximum(rowmax, jnp.max(scores, axis=-1))
        weights = jnp.where(vis, jnp.exp(scores - newmax[..., None]), jnp.float32(0.0))
        factor = jnp.exp(rowmax - newmax)
        total = total * factor + jnp.sum(weights, axis=-1)
        rounded = weights.astype(jnp.bfloat16)
        contrib = jnp.einsum(
            "tgns,sgh->tgnh",
            rounded,
            vblk.reshape(tok_rows, groups, HEAD_SIZE),
            preferred_element_type=jnp.float32,
        )
        accum = accum * factor[..., None] + contrib
        return (newmax, total, accum)

    def attend(state, kblk, vblk, sblk, kstart):
        return work(state, kblk, vblk, sblk, kstart)

    state = (
        jnp.full((tok_rows, groups, QPG), -1e30, jnp.float32),
        jnp.zeros((tok_rows, groups, QPG), jnp.float32),
        jnp.zeros((tok_rows, groups, QPG, HEAD_SIZE), jnp.float32),
    )
    state = attend(state, keys, values, doc_ids, here * tok_rows)

    def chain_step(depth, carry):
        st, kblk, vblk, sblk = carry
        kblk, vblk, sblk = passed_along((kblk, vblk, sblk), "ctx", 1)
        st = attend(st, kblk, vblk, sblk, (here - depth) * tok_rows)
        return (st, kblk, vblk, sblk)

    state = lax.fori_loop(1, reach + 1, chain_step, (state, keys, values, doc_ids))[0]
    rowmax, total, accum = state
    attn = (
        (accum / total[..., None]).astype(jnp.bfloat16).reshape(tok_rows, groups * QPG * HEAD_SIZE)
    )
    partial_sums = jnp.dot(
        attn,
        lax.all_gather(out_weight, "ctx", axis=1, tiled=True),
        preferred_element_type=jnp.float32,
    )
    return lax.psum_scatter(
        partial_sums.astype(jnp.bfloat16), "heads", scatter_dimension=1, tiled=True
    )


def solution(mesh):
    in_specs = (
        P("ctx", "heads"),
        P("ctx", "heads"),
        P("ctx", "heads"),
        P("ctx"),
        P("heads", "ctx"),
    )
    out_specs = P("ctx", "heads")

    def run(queries, keys, values, doc_ids, out_weight):
        n_ctx, n_heads = mesh.shape["ctx"], mesh.shape["heads"]
        local = body
        if fits_fused(n_ctx, n_heads, queries, keys, out_weight):
            local = functools.partial(fused_body, n_ctx, n_heads)
        return jax.shard_map(
            local, mesh=mesh, in_specs=in_specs, out_specs=out_specs, check_vma=False
        )(queries, keys, values, doc_ids, out_weight)

    return run
```

```python
import functools
import math

import jax
import jax.numpy as jnp
from jax import lax
from jax.experimental import pallas as pl
from jax.experimental.pallas import tpu as pltpu
from jax.sharding import PartitionSpec as P

HEAD_SIZE = 128
LOOKBACK_WINDOW = 4096
QPG = 4


PLANE = 4
DOC_ROWS = 16
MESH = pl.DeviceIdType.MESH


def fused_kernel(
    planes, n_heads, groups, tok, wcols,
    q_ref, kv_hbm, w_hbm, out_ref,
    kvbuf, wbuf, abuf, acc, rowmax, total, bias, xsend, xrecv, keep, rsend, obuf,
    local_sem, kv_recv, kvz_send, kvp_send, kvf_send,
    w_recv, w_right, w_left, a_recv, a_send, a_fwd,
    x_send, x_recv, o_send, o_recv,
):
    h = lax.axis_index("heads")
    c = lax.axis_index("ctx")
    z = c // PLANE
    p = c % PLANE
    core = p % 2
    row = p // 2
    mate = p + 1 - 2 * core
    across = (p + 2) % PLANE
    diag = (mate + 2) % PLANE
    last = planes - 1
    kdim = groups * HEAD_SIZE
    span = QPG * groups
    per_half = planes // n_heads
    half = wcols // 2

    def in_plane(other):
        return (h, z * PLANE + other)

    up = (h, c + PLANE)
    down = (h, c - PLANE)

    def copy(src, dst, send, recv, dev):
        return pltpu.make_async_remote_copy(
            src_ref=src, dst_ref=dst, send_sem=send, recv_sem=recv,
            device_id=dev, device_id_type=MESH,
        )

    def kv_up(d):
        return copy(kvbuf.at[d, p], kvbuf.at[d + 1, p], kvz_send.at[d], kv_recv.at[d + 1, p], up)

    def kv_side(d, which):
        dev = in_plane(mate if which == 0 else across)
        return copy(kvbuf.at[d, p], kvbuf.at[d, p], kvp_send.at[d, which], kv_recv.at[d, p], dev)

    def kv_forward(d):
        return copy(
            kvbuf.at[d, across], kvbuf.at[d, across], kvf_send.at[d], kv_recv.at[d, across],
            in_plane(mate),
        )

    def kv_wait(d, who):
        copy(
            kvbuf.at[d, who], kvbuf.at[d, who], kvf_send.at[d], kv_recv.at[d, who], in_plane(mate)
        ).wait_recv()

    def w_up(j, s):
        ref = wbuf.at[j, s]
        return copy(ref, ref, w_right.at[j, s], w_recv.at[j, s], up)

    def w_down(j, s):
        ref = wbuf.at[j, s]
        return copy(ref, ref, w_left.at[j, s], w_recv.at[j, s], down)

    def w_wait(j, s):
        ref = wbuf.at[j, s]
        copy(ref, ref, w_left.at[j, s], w_recv.at[j, s], in_plane(mate)).wait_recv()

    def w_from_above(j):
        for s in range(2):
            w_wait(j, s)

            @pl.when(z > 0)
            def _():
                w_down(j, s).start()

    def w_from_below(j):
        for s in range(2):
            w_wait(j, s)

            @pl.when(z < last)
            def _():
                w_up(j, s).start()

    def target(k):
        return jnp.where(k == 0, across, jnp.where(k == 1, diag, jnp.where(k == 2, mate, p)))

    def a_side(which):
        dev = in_plane(mate if which == 0 else across)
        return copy(abuf.at[p], abuf.at[p], a_send.at[which], a_recv.at[p], dev)

    def a_forward():
        return copy(abuf.at[across], abuf.at[across], a_fwd, a_recv.at[across], in_plane(mate))

    def a_wait(who):
        copy(abuf.at[who], abuf.at[who], a_fwd, a_recv.at[who], in_plane(mate)).wait_recv()

    def x_copy(u, pp):
        return copy(
            xsend.at[u, pp], xrecv.at[u, pp], x_send.at[u, pp], x_recv.at[u, pp], (1 - h, c)
        )

    def o_copy(u, pp):
        return copy(
            rsend.at[u, pp], obuf.at[u, p], o_send.at[u, pp], o_recv.at[u, p], in_plane(pp)
        )

    kv_in = pltpu.make_async_copy(kv_hbm, kvbuf.at[0, p], local_sem.at[0])
    w_in = [
        pltpu.make_async_copy(
            w_hbm.at[:, s * half : (s + 1) * half], wbuf.at[z, s], local_sem.at[1 + s]
        )
        for s in range(2)
    ]
    kv_in.start()
    w_in[0].start()
    w_in[1].start()

    barrier = pltpu.get_barrier_semaphore()
    for dev in (in_plane(mate), in_plane(across), in_plane(diag), (1 - h, c)):
        pl.semaphore_signal(barrier, inc=1, device_id=dev, device_id_type=MESH)

    @pl.when(z < last)
    def _():
        pl.semaphore_signal(barrier, inc=1, device_id=up, device_id_type=MESH)

    @pl.when(z > 0)
    def _():
        pl.semaphore_signal(barrier, inc=1, device_id=down, device_id_type=MESH)

    pl.semaphore_wait(barrier, 4 + jnp.minimum(z, 1) + jnp.minimum(last - z, 1))

    kv_in.wait()

    @pl.when(z < last)
    def _():
        kv_up(0).start()

    @pl.when(row == 0)
    def _():
        kv_side(0, 1).start()

    @pl.when(core == 0)
    def _():
        kv_side(0, 0).start()

    w_in[0].wait()
    w_in[1].wait()

    @pl.when(z > 0)
    def _():
        w_down(z, 0).start()
        w_down(z, 1).start()

    factor = HEAD_SIZE ** (-0.5) * math.log2(math.e)

    def docs_of(block):
        return block[tok : tok + DOC_ROWS, 0:tok].astype(jnp.float32)[0:1, :]

    def attend(d, who, first):
        block = kvbuf.at[d, who]
        kdoc = jnp.broadcast_to(docs_of(block), (tok, tok)).T
        vis = kdoc == docs_of(kvbuf.at[0, p])
        if first:
            kpos = lax.broadcasted_iota(jnp.int32, (tok, tok), 0)
            qpos = lax.broadcasted_iota(jnp.int32, (tok, tok), 1)
            vis = vis & (kpos <= qpos)
        bias[...] = jnp.where(vis, jnp.float32(0.0), jnp.float32(-1e30))

        def group(g, carry):
            keys = block[0:tok, pl.ds(pl.multiple_of(g * HEAD_SIZE, HEAD_SIZE), HEAD_SIZE)]
            vals = block[0:tok, pl.ds(pl.multiple_of(kdim + g * HEAD_SIZE, HEAD_SIZE), HEAD_SIZE)]
            for n in range(QPG):
                head = g * QPG + n
                qs = q_ref[:, pl.ds(pl.multiple_of(head * HEAD_SIZE, HEAD_SIZE), HEAD_SIZE)]
                scores = lax.dot_general(
                    keys, qs, (((1,), (1,)), ((), ())), preferred_element_type=jnp.float32
                ) + bias[...]
                top = jnp.max(scores, axis=0, keepdims=True)
                if not first:
                    old = rowmax[head]
                    top = jnp.maximum(old, top)
                weights = jnp.exp2((scores - top) * factor)
                sums = jnp.sum(weights, axis=0, keepdims=True)
                contrib = lax.dot_general(
                    vals, weights.astype(jnp.bfloat16), (((0,), (0,)), ((), ())),
                    preferred_element_type=jnp.float32,
                )
                if first:
                    total[head] = sums
                    acc[head] = contrib
                else:
                    shrink = jnp.exp2((old - top) * factor)
                    total[head] = total[head] * shrink + sums
                    acc[head] = acc[head] * shrink + contrib
                rowmax[head] = top
            return carry

        lax.fori_loop(0, groups, group, 0)

    attend(0, p, True)

    @pl.when(z > 0)
    def _():
        kv_wait(1, p)

        @pl.when(z < last)
        def _():
            kv_up(1).start()

        kv_side(1, 1).start()
        kv_side(1, 0).start()

    @pl.when(z < last)
    def _():
        w_up(z, 0).start()
        w_up(z, 1).start()

    @pl.when(row == 1)
    def _():
        kv_wait(0, across)
        kv_forward(0).start()

    @pl.when(core == 1)
    def _():
        kv_wait(0, mate)

    @pl.when(row == 1)
    def _():
        kv_wait(0, diag)

    def block_loop(d, lo, hi):
        def one(who, carry):
            attend(d, who, False)
            return carry

        lax.fori_loop(lo, hi, one, 0)

    block_loop(0, 0, p)

    @pl.when(z > 0)
    def _():
        kv_wait(1, across)
        kv_forward(1).start()

    @pl.when(z > 1)
    def _():
        kv_wait(2, p)

        @pl.when(row == 1)
        def _():
            kv_side(2, 1).start()

        @pl.when(core == 1)
        def _():
            kv_side(2, 0).start()

    @pl.when(z < last)
    def _():
        w_from_above(z + 1)

    @pl.when(z > 0)
    def _():
        kv_wait(1, mate)
        kv_wait(1, diag)
        block_loop(1, 0, PLANE)

    @pl.when(z > 0)
    def _():
        w_from_below(z - 1)

    @pl.when(z + 2 < planes)
    def _():
        w_from_above(z + 2)

    @pl.when(z > 1)
    def _():
        @pl.when(row == 0)
        def _():
            kv_wait(2, across)
            kv_forward(2).start()

        @pl.when(core == 0)
        def _():
            kv_wait(2, mate)

        @pl.when(row == 0)
        def _():
            kv_wait(2, diag)

        block_loop(2, p, PLANE)

    def finish_head(head, carry):
        cols = pl.ds(pl.multiple_of(head * HEAD_SIZE, HEAD_SIZE), HEAD_SIZE)
        abuf[p, :, cols] = (acc[head] / total[head]).T.astype(jnp.bfloat16)
        return carry

    lax.fori_loop(0, span, finish_head, 0)
    a_side(1).start()
    a_side(0).start()

    @pl.when(z > 1)
    def _():
        w_from_below(z - 2)

    a_wait(across)
    a_forward().start()
    a_wait(mate)
    a_wait(diag)

    def plane_of(i):
        dist = (i + 1) // 2
        return z + dist * (2 * (i % 2) - 1)

    def exists(j):
        return (j >= 0) & (j < planes)

    def place(u, pp, part):
        j = u // 2
        mine = (j // per_half) == h
        uu = u % (2 * per_half)

        @pl.when(mine)
        def _():
            keep[uu, pp] = part

        @pl.when(jnp.logical_not(mine))
        def _():
            xsend[uu, pp] = part.astype(jnp.bfloat16)
            x_copy(uu, pp).start()

    def project(i):
        j = plane_of(i)

        @pl.when(exists(j))
        def _():
            @pl.when(i >= 5)
            def _():
                w_wait(j, 0)
                w_wait(j, 1)

            def rows(k, carry):
                pp = target(k)
                both = jnp.concatenate([wbuf[j, 0], wbuf[j, 1]], axis=1)
                part = jnp.dot(abuf[pp], both, preferred_element_type=jnp.float32)
                place(2 * j, pp, part[:, :half])
                place(2 * j + 1, pp, part[:, half:])
                return carry

            lax.fori_loop(0, PLANE, rows, 0)

    def project_half(i, s):
        j = plane_of(i)

        @pl.when(exists(j))
        def _():
            w_wait(j, s)

            def rows(k, carry):
                pp = target(k)
                part = jnp.dot(abuf[pp], wbuf[j, s], preferred_element_type=jnp.float32)
                place(2 * j + s, pp, part)
                return carry

            lax.fori_loop(0, PLANE, rows, 0)

    def finish(i, s):
        j = plane_of(i)

        @pl.when(exists(j) & ((j // per_half) == h))
        def _():
            u = (2 * j + s) % (2 * per_half)

            def rows(k, carry):
                pp = target(k)
                x_copy(u, pp).wait_recv()
                done = (keep[u, pp] + xrecv[u, pp].astype(jnp.float32)).astype(jnp.bfloat16)

                @pl.when(pp == p)
                def _():
                    out_ref[:, column(u, p)] = done

                @pl.when(pp != p)
                def _():
                    rsend[u, pp] = done
                    o_copy(u, pp).start()

                return carry

            lax.fori_loop(0, PLANE, rows, 0)

    def column(u, src):
        return pl.ds(pl.multiple_of(((u // 2) * PLANE + src) * wcols + (u % 2) * half, half), half)

    steps = 2 * planes - 1

    def project_step(i, carry):
        project(i)
        return carry

    def finish_step(k, carry):
        finish(k // 2, k % 2)
        return carry

    lax.fori_loop(0, steps - 1, project_step, 0)
    def far_project(s, carry):
        project_half(steps - 1, s)
        return carry

    lax.fori_loop(0, 2, far_project, 0)
    lax.fori_loop(0, 2 * steps, finish_step, 0)

    def collect(k, carry):
        u = k // PLANE
        src = k % PLANE

        @pl.when(src != p)
        def _():
            copy(
                obuf.at[u, src], obuf.at[u, src], o_send.at[u, src], o_recv.at[u, src],
                in_plane(mate),
            ).wait_recv()
            out_ref[:, column(u, src)] = obuf[u, src]
            o_copy(u, src).wait_send()

        x_copy(u, src).wait_send()
        return carry

    lax.fori_loop(0, 2 * per_half * PLANE, collect, 0)

    a_side(0).wait_send()
    a_side(1).wait_send()
    a_forward().wait_send()

    def w_drain(j, carry):
        @pl.when((j <= z) & (z < last))
        def _():
            w_up(j, 0).wait_send()
            w_up(j, 1).wait_send()

        @pl.when((j >= z) & (z > 0))
        def _():
            w_down(j, 0).wait_send()
            w_down(j, 1).wait_send()

        return carry

    lax.fori_loop(0, planes, w_drain, 0)

    @pl.when(z < last)
    def _():
        kv_up(0).wait_send()

        @pl.when(z > 0)
        def _():
            kv_up(1).wait_send()

    @pl.when(row == 0)
    def _():
        kv_side(0, 1).wait_send()

    @pl.when(core == 0)
    def _():
        kv_side(0, 0).wait_send()

    @pl.when(row == 1)
    def _():
        kv_forward(0).wait_send()

    @pl.when(z > 0)
    def _():
        kv_side(1, 0).wait_send()
        kv_side(1, 1).wait_send()
        kv_forward(1).wait_send()

    @pl.when(z > 1)
    def _():
        @pl.when(row == 1)
        def _():
            kv_side(2, 1).wait_send()

        @pl.when(core == 1)
        def _():
            kv_side(2, 0).wait_send()

        @pl.when(row == 0)
        def _():
            kv_forward(2).wait_send()


def fused_body(n_ctx, n_heads, queries, keys, values, doc_ids, out_weight):
    tok, qcols = queries.shape
    kdim = keys.shape[1]
    groups = kdim // HEAD_SIZE
    krows, wcols = out_weight.shape
    planes = n_ctx // PLANE
    span = QPG * groups
    per_half = planes // n_heads
    width = 2 * kdim
    docs = jnp.broadcast_to(
        jnp.pad(doc_ids.astype(jnp.bfloat16), (0, width - tok))[None, :], (DOC_ROWS, width)
    )
    kv = jnp.concatenate([jnp.concatenate([keys, values], axis=1), docs], axis=0)
    bf, f32 = jnp.bfloat16, jnp.float32
    dma = pltpu.SemaphoreType.DMA
    return pl.pallas_call(
        functools.partial(fused_kernel, planes, n_heads, groups, tok, wcols),
        out_shape=jax.ShapeDtypeStruct((tok, per_half * PLANE * wcols), bf),
        in_specs=[
            pl.BlockSpec(memory_space=pltpu.VMEM),
            pl.BlockSpec(memory_space=pl.ANY),
            pl.BlockSpec(memory_space=pl.ANY),
        ],
        out_specs=pl.BlockSpec(memory_space=pltpu.VMEM),
        scratch_shapes=[
            pltpu.VMEM((3, PLANE, tok + DOC_ROWS, width), bf),
            pltpu.VMEM((planes, 2, krows, wcols // 2), bf),
            pltpu.VMEM((PLANE, tok, krows), bf),
            pltpu.VMEM((span, HEAD_SIZE, tok), f32),
            pltpu.VMEM((span, 1, tok), f32),
            pltpu.VMEM((span, 1, tok), f32),
            pltpu.VMEM((tok, tok), f32),
            pltpu.VMEM((2 * per_half, PLANE, tok, wcols // 2), bf),
            pltpu.VMEM((2 * per_half, PLANE, tok, wcols // 2), bf),
            pltpu.VMEM((2 * per_half, PLANE, tok, wcols // 2), f32),
            pltpu.VMEM((2 * per_half, PLANE, tok, wcols // 2), bf),
            pltpu.VMEM((2 * per_half, PLANE, tok, wcols // 2), bf),
            dma((3,)),
            dma((3, PLANE)),
            dma((2,)),
            dma((3, 2)),
            dma((3,)),
            dma((planes, 2)),
            dma((planes, 2)),
            dma((planes, 2)),
            dma((PLANE,)),
            dma((2,)),
            dma,
            dma((2 * per_half, PLANE)),
            dma((2 * per_half, PLANE)),
            dma((2 * per_half, PLANE)),
            dma((2 * per_half, PLANE)),
        ],
        compiler_params=pltpu.CompilerParams(
            collective_id=0, has_side_effects=True, vmem_limit_bytes=56 * 1024 * 1024
        ),
    )(queries, kv, out_weight)


def fits_fused(n_ctx, n_heads, queries, keys, out_weight):
    tokens = queries.shape[0]
    tok = tokens // n_ctx
    reach = min(LOOKBACK_WINDOW, tokens // 2)
    return (
        n_heads == 2
        and n_ctx % PLANE == 0
        and n_ctx // PLANE == 4
        and tok == 2 * HEAD_SIZE
        and reach == 2 * PLANE * tok
        and reach < LOOKBACK_WINDOW
        and 2 * keys.shape[1] // n_heads >= tok
        and (out_weight.shape[1] // n_ctx) % 256 == 0
        and keys.shape[1] // n_heads % HEAD_SIZE == 0
    )


def passed_along(block, axis, distance):
    devices = range(lax.axis_size(axis))
    route = [(i - distance, i) for i in devices if i - distance in devices]
    return lax.ppermute(block, axis, route)


def body(queries, keys, values, doc_ids, out_weight):
    tok_rows = queries.shape[0]
    groups = keys.shape[1] // HEAD_SIZE
    scale = HEAD_SIZE ** (-0.5)
    q_local = queries.reshape(tok_rows, groups, QPG, HEAD_SIZE)
    here = lax.axis_index("ctx")
    qpos = here * tok_rows + jnp.arange(tok_rows, dtype=jnp.int32)
    reach = LOOKBACK_WINDOW // tok_rows

    def work(state, kblk, vblk, sblk, kstart):
        rowmax, total, accum = state
        scores = (
            jnp.einsum(
                "tgnh,sgh->tgns",
                q_local,
                kblk.reshape(tok_rows, groups, HEAD_SIZE),
                preferred_element_type=jnp.float32,
            )
            * scale
        )
        kpos = kstart + jnp.arange(tok_rows, dtype=jnp.int32)
        vis = (
            (kpos[None, :] <= qpos[:, None])
            & (qpos[:, None] - kpos[None, :] < LOOKBACK_WINDOW)
            & (kpos[None, :] >= 0)
            & (doc_ids[:, None] == sblk[None, :])
        )
        vis = vis[:, None, None, :]
        scores = jnp.where(vis, scores, jnp.float32(-1e30))
        newmax = jnp.maximum(rowmax, jnp.max(scores, axis=-1))
        weights = jnp.where(vis, jnp.exp(scores - newmax[..., None]), jnp.float32(0.0))
        factor = jnp.exp(rowmax - newmax)
        total = total * factor + jnp.sum(weights, axis=-1)
        rounded = weights.astype(jnp.bfloat16)
        contrib = jnp.einsum(
            "tgns,sgh->tgnh",
            rounded,
            vblk.reshape(tok_rows, groups, HEAD_SIZE),
            preferred_element_type=jnp.float32,
        )
        accum = accum * factor[..., None] + contrib
        return (newmax, total, accum)

    def attend(state, kblk, vblk, sblk, kstart):
        return work(state, kblk, vblk, sblk, kstart)

    state = (
        jnp.full((tok_rows, groups, QPG), -1e30, jnp.float32),
        jnp.zeros((tok_rows, groups, QPG), jnp.float32),
        jnp.zeros((tok_rows, groups, QPG, HEAD_SIZE), jnp.float32),
    )
    state = attend(state, keys, values, doc_ids, here * tok_rows)

    def chain_step(depth, carry):
        st, kblk, vblk, sblk = carry
        kblk, vblk, sblk = passed_along((kblk, vblk, sblk), "ctx", 1)
        st = attend(st, kblk, vblk, sblk, (here - depth) * tok_rows)
        return (st, kblk, vblk, sblk)

    state = lax.fori_loop(1, reach + 1, chain_step, (state, keys, values, doc_ids))[0]
    rowmax, total, accum = state
    attn = (
        (accum / total[..., None]).astype(jnp.bfloat16).reshape(tok_rows, groups * QPG * HEAD_SIZE)
    )
    partial_sums = jnp.dot(
        attn,
        lax.all_gather(out_weight, "ctx", axis=1, tiled=True),
        preferred_element_type=jnp.float32,
    )
    return lax.psum_scatter(
        partial_sums.astype(jnp.bfloat16), "heads", scatter_dimension=1, tiled=True
    )


def solution(mesh):
    in_specs = (
        P("ctx", "heads"),
        P("ctx", "heads"),
        P("ctx", "heads"),
        P("ctx"),
        P("heads", "ctx"),
    )
    out_specs = P("ctx", "heads")

    def run(queries, keys, values, doc_ids, out_weight):
        n_ctx, n_heads = mesh.shape["ctx"], mesh.shape["heads"]
        local = body
        if fits_fused(n_ctx, n_heads, queries, keys, out_weight):
            local = functools.partial(fused_body, n_ctx, n_heads)
        return jax.shard_map(
            local, mesh=mesh, in_specs=in_specs, out_specs=out_specs, check_vma=False
        )(queries, keys, values, doc_ids, out_weight)

    return run
```

```python
import functools
import math

import jax
import jax.numpy as jnp
from jax import lax
from jax.experimental import pallas as pl
from jax.experimental.pallas import tpu as pltpu
from jax.sharding import PartitionSpec as P

HEAD_SIZE = 128
LOOKBACK_WINDOW = 4096
QPG = 4


PLANE = 4
DOC_ROWS = 16
MESH = pl.DeviceIdType.MESH


def fused_kernel(
    planes, n_heads, groups, tok, wcols,
    q_ref, kv_hbm, w_hbm, out_ref,
    kvbuf, wbuf, abuf, acc, rowmax, total, bias, xsend, xrecv, keep, rsend, obuf,
    local_sem, kv_recv, kvz_send, kvp_send, kvf_send,
    w_recv, w_right, w_left, a_recv, a_send, a_fwd,
    x_send, x_recv, o_send, o_recv,
):
    h = lax.axis_index("heads")
    c = lax.axis_index("ctx")
    z = c // PLANE
    p = c % PLANE
    core = p % 2
    row = p // 2
    mate = p + 1 - 2 * core
    across = (p + 2) % PLANE
    diag = (mate + 2) % PLANE
    last = planes - 1
    kdim = groups * HEAD_SIZE
    span = QPG * groups
    per_half = planes // n_heads
    half = wcols // 2

    def in_plane(other):
        return (h, z * PLANE + other)

    up = (h, c + PLANE)
    down = (h, c - PLANE)

    def copy(src, dst, send, recv, dev):
        return pltpu.make_async_remote_copy(
            src_ref=src, dst_ref=dst, send_sem=send, recv_sem=recv,
            device_id=dev, device_id_type=MESH,
        )

    def kv_up(d):
        return copy(kvbuf.at[d, p], kvbuf.at[d + 1, p], kvz_send.at[d], kv_recv.at[d + 1, p], up)

    def kv_side(d, which):
        dev = in_plane(mate if which == 0 else across)
        return copy(kvbuf.at[d, p], kvbuf.at[d, p], kvp_send.at[d, which], kv_recv.at[d, p], dev)

    def kv_forward(d):
        return copy(
            kvbuf.at[d, across], kvbuf.at[d, across], kvf_send.at[d], kv_recv.at[d, across],
            in_plane(mate),
        )

    def kv_wait(d, who):
        copy(
            kvbuf.at[d, who], kvbuf.at[d, who], kvf_send.at[d], kv_recv.at[d, who], in_plane(mate)
        ).wait_recv()

    def w_up(j, s):
        ref = wbuf.at[j, s]
        return copy(ref, ref, w_right.at[j, s], w_recv.at[j, s], up)

    def w_down(j, s):
        ref = wbuf.at[j, s]
        return copy(ref, ref, w_left.at[j, s], w_recv.at[j, s], down)

    def w_wait(j, s):
        ref = wbuf.at[j, s]
        copy(ref, ref, w_left.at[j, s], w_recv.at[j, s], in_plane(mate)).wait_recv()

    def w_from_above(j):
        for s in range(2):
            w_wait(j, s)

            @pl.when(z > 0)
            def _():
                w_down(j, s).start()

    def w_from_below(j):
        for s in range(2):
            w_wait(j, s)

            @pl.when(z < last)
            def _():
                w_up(j, s).start()

    def target(k):
        return jnp.where(k == 0, across, jnp.where(k == 1, diag, jnp.where(k == 2, mate, p)))

    def a_side(which):
        dev = in_plane(mate if which == 0 else across)
        return copy(abuf.at[p], abuf.at[p], a_send.at[which], a_recv.at[p], dev)

    def a_forward():
        return copy(abuf.at[across], abuf.at[across], a_fwd, a_recv.at[across], in_plane(mate))

    def a_wait(who):
        copy(abuf.at[who], abuf.at[who], a_fwd, a_recv.at[who], in_plane(mate)).wait_recv()

    def x_copy(u, pp):
        return copy(
            xsend.at[u, pp], xrecv.at[u, pp], x_send.at[u, pp], x_recv.at[u, pp], (1 - h, c)
        )

    def o_copy(u, pp):
        return copy(
            rsend.at[u, pp], obuf.at[u, p], o_send.at[u, pp], o_recv.at[u, p], in_plane(pp)
        )

    kv_in = pltpu.make_async_copy(kv_hbm, kvbuf.at[0, p], local_sem.at[0])
    w_in = [
        pltpu.make_async_copy(
            w_hbm.at[:, s * half : (s + 1) * half], wbuf.at[z, s], local_sem.at[1 + s]
        )
        for s in range(2)
    ]
    kv_in.start()
    w_in[0].start()
    w_in[1].start()

    barrier = pltpu.get_barrier_semaphore()
    for dev in (in_plane(mate), in_plane(across), in_plane(diag), (1 - h, c)):
        pl.semaphore_signal(barrier, inc=1, device_id=dev, device_id_type=MESH)

    @pl.when(z < last)
    def _():
        pl.semaphore_signal(barrier, inc=1, device_id=up, device_id_type=MESH)

    @pl.when(z > 0)
    def _():
        pl.semaphore_signal(barrier, inc=1, device_id=down, device_id_type=MESH)

    pl.semaphore_wait(barrier, 4 + jnp.minimum(z, 1) + jnp.minimum(last - z, 1))

    kv_in.wait()

    @pl.when(z < last)
    def _():
        kv_up(0).start()

    @pl.when(row == 0)
    def _():
        kv_side(0, 1).start()

    @pl.when(core == 0)
    def _():
        kv_side(0, 0).start()

    w_in[0].wait()
    w_in[1].wait()

    @pl.when(z > 0)
    def _():
        w_down(z, 0).start()
        w_down(z, 1).start()

    factor = HEAD_SIZE ** (-0.5) * math.log2(math.e)

    def docs_of(block):
        return block[tok : tok + DOC_ROWS, 0:tok].astype(jnp.float32)[0:1, :]

    def attend(d, who, first):
        block = kvbuf.at[d, who]
        kdoc = jnp.broadcast_to(docs_of(block), (tok, tok)).T
        vis = kdoc == docs_of(kvbuf.at[0, p])
        if first:
            kpos = lax.broadcasted_iota(jnp.int32, (tok, tok), 0)
            qpos = lax.broadcasted_iota(jnp.int32, (tok, tok), 1)
            vis = vis & (kpos <= qpos)
        bias[...] = jnp.where(vis, jnp.float32(0.0), jnp.float32(-1e30))

        def group(g, carry):
            keys = block[0:tok, pl.ds(pl.multiple_of(g * HEAD_SIZE, HEAD_SIZE), HEAD_SIZE)]
            vals = block[0:tok, pl.ds(pl.multiple_of(kdim + g * HEAD_SIZE, HEAD_SIZE), HEAD_SIZE)]
            for n in range(QPG):
                head = g * QPG + n
                qs = q_ref[:, pl.ds(pl.multiple_of(head * HEAD_SIZE, HEAD_SIZE), HEAD_SIZE)]
                scores = lax.dot_general(
                    keys, qs, (((1,), (1,)), ((), ())), preferred_element_type=jnp.float32
                ) + bias[...]
                top = jnp.max(scores, axis=0, keepdims=True)
                if not first:
                    old = rowmax[head]
                    top = jnp.maximum(old, top)
                weights = jnp.exp2((scores - top) * factor)
                sums = jnp.sum(weights, axis=0, keepdims=True)
                contrib = lax.dot_general(
                    vals, weights.astype(jnp.bfloat16), (((0,), (0,)), ((), ())),
                    preferred_element_type=jnp.float32,
                )
                if first:
                    total[head] = sums
                    acc[head] = contrib
                else:
                    shrink = jnp.exp2((old - top) * factor)
                    total[head] = total[head] * shrink + sums
                    acc[head] = acc[head] * shrink + contrib
                rowmax[head] = top
            return carry

        lax.fori_loop(0, groups, group, 0)

    attend(0, p, True)

    @pl.when(z > 0)
    def _():
        kv_wait(1, p)

        @pl.when(z < last)
        def _():
            kv_up(1).start()

        kv_side(1, 1).start()
        kv_side(1, 0).start()

    @pl.when(z < last)
    def _():
        w_up(z, 0).start()
        w_up(z, 1).start()

    @pl.when(row == 1)
    def _():
        kv_wait(0, across)
        kv_forward(0).start()

    @pl.when(core == 1)
    def _():
        kv_wait(0, mate)

    @pl.when(row == 1)
    def _():
        kv_wait(0, diag)

    def block_loop(d, lo, hi):
        def one(who, carry):
            attend(d, who, False)
            return carry

        lax.fori_loop(lo, hi, one, 0)

    block_loop(0, 0, p)

    @pl.when(z > 0)
    def _():
        kv_wait(1, across)
        kv_forward(1).start()

    @pl.when(z > 1)
    def _():
        kv_wait(2, p)

        @pl.when(row == 1)
        def _():
            kv_side(2, 1).start()

        @pl.when(core == 1)
        def _():
            kv_side(2, 0).start()

    @pl.when(z < last)
    def _():
        w_from_above(z + 1)

    @pl.when(z > 0)
    def _():
        kv_wait(1, mate)
        kv_wait(1, diag)
        block_loop(1, 0, PLANE)

    @pl.when((z > 0) & (z < last))
    def _():
        w_from_below(z - 1)

    @pl.when((z > 0) & (z + 2 < planes))
    def _():
        w_from_above(z + 2)

    @pl.when(z > 1)
    def _():
        @pl.when(row == 0)
        def _():
            kv_wait(2, across)
            kv_forward(2).start()

        @pl.when(core == 0)
        def _():
            kv_wait(2, mate)

        @pl.when(row == 0)
        def _():
            kv_wait(2, diag)

        block_loop(2, p, PLANE)

    def finish_head(head, carry):
        cols = pl.ds(pl.multiple_of(head * HEAD_SIZE, HEAD_SIZE), HEAD_SIZE)
        abuf[p, :, cols] = (acc[head] / total[head]).T.astype(jnp.bfloat16)
        return carry

    lax.fori_loop(0, span, finish_head, 0)
    a_side(1).start()
    a_side(0).start()

    @pl.when(z == last)
    def _():
        w_from_below(z - 1)

    @pl.when((z == 0) & (z + 2 < planes))
    def _():
        w_from_above(z + 2)

    @pl.when(z > 1)
    def _():
        w_from_below(z - 2)

    def plane_of(i):
        dist = (i + 1) // 2
        return z + dist * (2 * (i % 2) - 1)

    def exists(j):
        return (j >= 0) & (j < planes)

    def place(u, pp, part):
        j = u // 2
        mine = (j // per_half) == h
        uu = u % (2 * per_half)

        @pl.when(mine)
        def _():
            keep[uu, pp] = part

        @pl.when(jnp.logical_not(mine))
        def _():
            xsend[uu, pp] = part.astype(jnp.bfloat16)
            x_copy(uu, pp).start()

    def project(i, lo, hi):
        j = plane_of(i)

        @pl.when(exists(j))
        def _():
            @pl.when(i >= 5)
            def _():
                w_wait(j, 0)
                w_wait(j, 1)

            def rows(k, carry):
                pp = target(k)
                both = jnp.concatenate([wbuf[j, 0], wbuf[j, 1]], axis=1)
                part = jnp.dot(abuf[pp], both, preferred_element_type=jnp.float32)
                place(2 * j, pp, part[:, :half])
                place(2 * j + 1, pp, part[:, half:])
                return carry

            lax.fori_loop(lo, hi, rows, 0)

    def project_half(i, s):
        j = plane_of(i)

        @pl.when(exists(j))
        def _():
            w_wait(j, s)

            def rows(k, carry):
                pp = target(k)
                part = jnp.dot(abuf[pp], wbuf[j, s], preferred_element_type=jnp.float32)
                place(2 * j + s, pp, part)
                return carry

            lax.fori_loop(0, PLANE, rows, 0)

    def finish(i, s):
        j = plane_of(i)

        @pl.when(exists(j) & ((j // per_half) == h))
        def _():
            u = (2 * j + s) % (2 * per_half)

            def rows(k, carry):
                pp = target(k)
                x_copy(u, pp).wait_recv()
                done = (keep[u, pp] + xrecv[u, pp].astype(jnp.float32)).astype(jnp.bfloat16)

                @pl.when(pp == p)
                def _():
                    out_ref[:, column(u, p)] = done

                @pl.when(pp != p)
                def _():
                    rsend[u, pp] = done
                    o_copy(u, pp).start()

                return carry

            lax.fori_loop(0, PLANE, rows, 0)

    def column(u, src):
        return pl.ds(pl.multiple_of(((u // 2) * PLANE + src) * wcols + (u % 2) * half, half), half)

    steps = 2 * planes - 1

    def near_step(i, carry):
        project(i, 2, PLANE)
        return carry

    def across_step(i, carry):
        project(i, 0, 2)
        return carry

    def finish_step(k, carry):
        finish(k // 2, k % 2)
        return carry

    a_wait(mate)
    lax.fori_loop(0, steps - 2, near_step, 0)
    a_wait(across)
    a_forward().start()
    a_wait(diag)
    lax.fori_loop(0, steps - 2, across_step, 0)
    project(steps - 2, 0, PLANE)
    def far_project(s, carry):
        project_half(steps - 1, s)
        return carry

    lax.fori_loop(0, 2, far_project, 0)
    lax.fori_loop(0, 2 * steps, finish_step, 0)

    def collect(k, carry):
        u = k // PLANE
        src = k % PLANE

        @pl.when(src != p)
        def _():
            copy(
                obuf.at[u, src], obuf.at[u, src], o_send.at[u, src], o_recv.at[u, src],
                in_plane(mate),
            ).wait_recv()
            out_ref[:, column(u, src)] = obuf[u, src]
            o_copy(u, src).wait_send()

        x_copy(u, src).wait_send()
        return carry

    lax.fori_loop(0, 2 * per_half * PLANE, collect, 0)

    a_side(0).wait_send()
    a_side(1).wait_send()
    a_forward().wait_send()

    def w_drain(j, carry):
        @pl.when((j <= z) & (z < last))
        def _():
            w_up(j, 0).wait_send()
            w_up(j, 1).wait_send()

        @pl.when((j >= z) & (z > 0))
        def _():
            w_down(j, 0).wait_send()
            w_down(j, 1).wait_send()

        return carry

    lax.fori_loop(0, planes, w_drain, 0)

    @pl.when(z < last)
    def _():
        kv_up(0).wait_send()

        @pl.when(z > 0)
        def _():
            kv_up(1).wait_send()

    @pl.when(row == 0)
    def _():
        kv_side(0, 1).wait_send()

    @pl.when(core == 0)
    def _():
        kv_side(0, 0).wait_send()

    @pl.when(row == 1)
    def _():
        kv_forward(0).wait_send()

    @pl.when(z > 0)
    def _():
        kv_side(1, 0).wait_send()
        kv_side(1, 1).wait_send()
        kv_forward(1).wait_send()

    @pl.when(z > 1)
    def _():
        @pl.when(row == 1)
        def _():
            kv_side(2, 1).wait_send()

        @pl.when(core == 1)
        def _():
            kv_side(2, 0).wait_send()

        @pl.when(row == 0)
        def _():
            kv_forward(2).wait_send()


def fused_body(n_ctx, n_heads, queries, keys, values, doc_ids, out_weight):
    tok, qcols = queries.shape
    kdim = keys.shape[1]
    groups = kdim // HEAD_SIZE
    krows, wcols = out_weight.shape
    planes = n_ctx // PLANE
    span = QPG * groups
    per_half = planes // n_heads
    width = 2 * kdim
    docs = jnp.broadcast_to(
        jnp.pad(doc_ids.astype(jnp.bfloat16), (0, width - tok))[None, :], (DOC_ROWS, width)
    )
    kv = jnp.concatenate([jnp.concatenate([keys, values], axis=1), docs], axis=0)
    bf, f32 = jnp.bfloat16, jnp.float32
    dma = pltpu.SemaphoreType.DMA
    return pl.pallas_call(
        functools.partial(fused_kernel, planes, n_heads, groups, tok, wcols),
        out_shape=jax.ShapeDtypeStruct((tok, per_half * PLANE * wcols), bf),
        in_specs=[
            pl.BlockSpec(memory_space=pltpu.VMEM),
            pl.BlockSpec(memory_space=pl.ANY),
            pl.BlockSpec(memory_space=pl.ANY),
        ],
        out_specs=pl.BlockSpec(memory_space=pltpu.VMEM),
        scratch_shapes=[
            pltpu.VMEM((3, PLANE, tok + DOC_ROWS, width), bf),
            pltpu.VMEM((planes, 2, krows, wcols // 2), bf),
            pltpu.VMEM((PLANE, tok, krows), bf),
            pltpu.VMEM((span, HEAD_SIZE, tok), f32),
            pltpu.VMEM((span, 1, tok), f32),
            pltpu.VMEM((span, 1, tok), f32),
            pltpu.VMEM((tok, tok), f32),
            pltpu.VMEM((2 * per_half, PLANE, tok, wcols // 2), bf),
            pltpu.VMEM((2 * per_half, PLANE, tok, wcols // 2), bf),
            pltpu.VMEM((2 * per_half, PLANE, tok, wcols // 2), f32),
            pltpu.VMEM((2 * per_half, PLANE, tok, wcols // 2), bf),
            pltpu.VMEM((2 * per_half, PLANE, tok, wcols // 2), bf),
            dma((3,)),
            dma((3, PLANE)),
            dma((2,)),
            dma((3, 2)),
            dma((3,)),
            dma((planes, 2)),
            dma((planes, 2)),
            dma((planes, 2)),
            dma((PLANE,)),
            dma((2,)),
            dma,
            dma((2 * per_half, PLANE)),
            dma((2 * per_half, PLANE)),
            dma((2 * per_half, PLANE)),
            dma((2 * per_half, PLANE)),
        ],
        compiler_params=pltpu.CompilerParams(
            collective_id=0, has_side_effects=True, vmem_limit_bytes=56 * 1024 * 1024
        ),
    )(queries, kv, out_weight)


def fits_fused(n_ctx, n_heads, queries, keys, out_weight):
    tokens = queries.shape[0]
    tok = tokens // n_ctx
    reach = min(LOOKBACK_WINDOW, tokens // 2)
    return (
        n_heads == 2
        and n_ctx % PLANE == 0
        and n_ctx // PLANE == 4
        and tok == 2 * HEAD_SIZE
        and reach == 2 * PLANE * tok
        and reach < LOOKBACK_WINDOW
        and 2 * keys.shape[1] // n_heads >= tok
        and (out_weight.shape[1] // n_ctx) % 256 == 0
        and keys.shape[1] // n_heads % HEAD_SIZE == 0
    )


def passed_along(block, axis, distance):
    devices = range(lax.axis_size(axis))
    route = [(i - distance, i) for i in devices if i - distance in devices]
    return lax.ppermute(block, axis, route)


def body(queries, keys, values, doc_ids, out_weight):
    tok_rows = queries.shape[0]
    groups = keys.shape[1] // HEAD_SIZE
    scale = HEAD_SIZE ** (-0.5)
    q_local = queries.reshape(tok_rows, groups, QPG, HEAD_SIZE)
    here = lax.axis_index("ctx")
    qpos = here * tok_rows + jnp.arange(tok_rows, dtype=jnp.int32)
    reach = LOOKBACK_WINDOW // tok_rows

    def work(state, kblk, vblk, sblk, kstart):
        rowmax, total, accum = state
        scores = (
            jnp.einsum(
                "tgnh,sgh->tgns",
                q_local,
                kblk.reshape(tok_rows, groups, HEAD_SIZE),
                preferred_element_type=jnp.float32,
            )
            * scale
        )
        kpos = kstart + jnp.arange(tok_rows, dtype=jnp.int32)
        vis = (
            (kpos[None, :] <= qpos[:, None])
            & (qpos[:, None] - kpos[None, :] < LOOKBACK_WINDOW)
            & (kpos[None, :] >= 0)
            & (doc_ids[:, None] == sblk[None, :])
        )
        vis = vis[:, None, None, :]
        scores = jnp.where(vis, scores, jnp.float32(-1e30))
        newmax = jnp.maximum(rowmax, jnp.max(scores, axis=-1))
        weights = jnp.where(vis, jnp.exp(scores - newmax[..., None]), jnp.float32(0.0))
        factor = jnp.exp(rowmax - newmax)
        total = total * factor + jnp.sum(weights, axis=-1)
        rounded = weights.astype(jnp.bfloat16)
        contrib = jnp.einsum(
            "tgns,sgh->tgnh",
            rounded,
            vblk.reshape(tok_rows, groups, HEAD_SIZE),
            preferred_element_type=jnp.float32,
        )
        accum = accum * factor[..., None] + contrib
        return (newmax, total, accum)

    def attend(state, kblk, vblk, sblk, kstart):
        return work(state, kblk, vblk, sblk, kstart)

    state = (
        jnp.full((tok_rows, groups, QPG), -1e30, jnp.float32),
        jnp.zeros((tok_rows, groups, QPG), jnp.float32),
        jnp.zeros((tok_rows, groups, QPG, HEAD_SIZE), jnp.float32),
    )
    state = attend(state, keys, values, doc_ids, here * tok_rows)

    def chain_step(depth, carry):
        st, kblk, vblk, sblk = carry
        kblk, vblk, sblk = passed_along((kblk, vblk, sblk), "ctx", 1)
        st = attend(st, kblk, vblk, sblk, (here - depth) * tok_rows)
        return (st, kblk, vblk, sblk)

    state = lax.fori_loop(1, reach + 1, chain_step, (state, keys, values, doc_ids))[0]
    rowmax, total, accum = state
    attn = (
        (accum / total[..., None]).astype(jnp.bfloat16).reshape(tok_rows, groups * QPG * HEAD_SIZE)
    )
    partial_sums = jnp.dot(
        attn,
        lax.all_gather(out_weight, "ctx", axis=1, tiled=True),
        preferred_element_type=jnp.float32,
    )
    return lax.psum_scatter(
        partial_sums.astype(jnp.bfloat16), "heads", scatter_dimension=1, tiled=True
    )


def solution(mesh):
    in_specs = (
        P("ctx", "heads"),
        P("ctx", "heads"),
        P("ctx", "heads"),
        P("ctx"),
        P("heads", "ctx"),
    )
    out_specs = P("ctx", "heads")

    def run(queries, keys, values, doc_ids, out_weight):
        n_ctx, n_heads = mesh.shape["ctx"], mesh.shape["heads"]
        local = body
        if fits_fused(n_ctx, n_heads, queries, keys, out_weight):
            local = functools.partial(fused_body, n_ctx, n_heads)
        return jax.shard_map(
            local, mesh=mesh, in_specs=in_specs, out_specs=out_specs, check_vma=False
        )(queries, keys, values, doc_ids, out_weight)

    return run
```
